32 devices in a mesh: fields: 2 (over x), vel: 8 (over z, y), rows: 2 (over core).
Axes of the slice: x: 2, y: 2, z: 4, core: 2. Of those that a mesh axis runs over, the one named last changes fastest.
Arguments:
- images: float32 [16, 64, 4096], P(('fields', 'vel'), 'rows'), parts along dimension 0, may hold values from -6 to 6
- variance: float32 [16, 64, 4096], P(('fields', 'vel'), 'rows'), parts along dimension 0, may hold values from 0.5 to 2
- spread_kernel: float32 [21, 21], replicated, may hold values from 0.05 to 1
- shifts: int32 [576, 3, 2], P(('fields', 'vel')), parts along dimension 0, may hold values from -16 to 16, as said below
- epoch_owner: int32 [6], P('fields'), parts along dimension 0, may hold values from 0 to 7, as said below
- valid_rows: int32 [6, 2], P('fields'), parts along dimension 0, may hold values from 0 to 64, as said below
Outputs:
- likelihood: float32 [576, 64, 4096], P(('fields', 'vel'), 'rows'), parts along dimension 0
The draws below stay inside these ranges and needn't reach their ends.
There are 2 independent parts, one for each index of `fields`. The reference program is written for one: setup_inputs(seed, part) draws one part's arguments, and reference() takes and returns one part's arrays. A program takes and returns all parts, laid end to end along the dimension named above; an argument that names none is the same for every part. Nothing has to cross between parts.
Inputs may be any that keep to these rules, and one draw needn't show every extreme that they name: `shifts`: each entry lies in -16 to 16; both ends are taken in every draw. `epoch_owner`: the epochs are held by distinct slots. `valid_rows`: in each row the first entry is below the second; the first epoch starts at row 0 and the last ends at row 64.
All inputs are finite; a program needn't handle non-finite values.
Results may differ from the reference program's by a relative error of at most 0.0003.
Values sent between devices are 32-bit elements; how exact they have to be, the bound alone decides.
A program may use at most 128 MiB of HBM per device.

```python
import math
import jax
import jax.numpy as jnp
from jax import lax

COLS = 4096
KSIZE = 21
MAXS = 16
EPOCHS = 3
ROWS = 64
VELOCITIES = 288
SLOTS = 8


def draw_shifts(key, part):
    values = jax.random.randint(key, (VELOCITIES, EPOCHS, 2), -MAXS, MAXS + 1)
    values = values.at[0, EPOCHS - 1].set(MAXS)
    values = values.at[VELOCITIES - 1, 0].set(-MAXS)
    return values.astype(jnp.int32)


def draw_epoch_owner(key, part):
    return jax.random.permutation(key, SLOTS)[:EPOCHS].astype(jnp.int32)


def draw_valid_rows(key, part):
    lower_rows = jax.random.randint(jax.random.fold_in(key, 11), (EPOCHS,), 0, ROWS // 4)
    upper_rows = ROWS - jax.random.randint(jax.random.fold_in(key, 12), (EPOCHS,), 0, ROWS // 4)
    lower_rows = lower_rows.at[0].set(0)
    upper_rows = upper_rows.at[EPOCHS - 1].set(ROWS)
    return jnp.stack([lower_rows, upper_rows], axis=1).astype(jnp.int32)


def block_scale(key, extent, shards, low, high):
    def one(axis_at, blocks):
        heights = jax.random.uniform(jax.random.fold_in(jax.random.fold_in(key, 6), axis_at), (blocks,), jnp.float32, low / len(shards), high / len(shards))
        return jnp.repeat(jnp.exp(heights), extent[axis_at] // blocks).reshape((-1,) + (1,) * (len(extent) - axis_at - 1))

    loudness = one(*shards[0])
    for cut in shards[1:]:
        loudness = loudness * one(*cut)
    return loudness


def normal_values(rng, shape, deviation, most, pieces=(), kind=jnp.bfloat16):
    array = deviation * jax.random.normal(rng, shape, jnp.float32)
    if pieces:
        array = array * block_scale(rng, shape, pieces, -0.22, 0.18)
    return jnp.clip(array, -most, most).astype(kind)


def setup_inputs(seed: int = 0, part: int = 0) -> dict:
    arg_keys = jax.random.split(jax.random.key(seed), 7)
    part_keys = jax.random.split(jax.random.fold_in(arg_keys[6], part), 7)
    images = normal_values(part_keys[0], (SLOTS, ROWS, COLS), 1.0, 6.0, ((0, 8), (1, 2)), jnp.float32)
    variance = jnp.clip(0.5 + 1.5 * jax.random.uniform(part_keys[1], (SLOTS, ROWS, COLS), jnp.float32) ** block_scale(part_keys[1], (SLOTS, ROWS, COLS), ((0, 8), (1, 2)), -0.2, 0.2), 0.5, 2.0)
    spread_kernel = jnp.clip(jnp.exp(jax.random.uniform(arg_keys[2], (KSIZE, KSIZE), jnp.float32, math.log(0.05), math.log(1.0))), 0.05, 1.0)
    shifts = draw_shifts(jax.random.fold_in(jax.random.fold_in(arg_keys[6], part), 71), part)
    epoch_owner = draw_epoch_owner(jax.random.fold_in(jax.random.fold_in(arg_keys[6], part), 71), part)
    valid_rows = draw_valid_rows(jax.random.fold_in(jax.random.fold_in(arg_keys[6], part), 71), part)
    return {"images": images, "variance": variance, "spread_kernel": spread_kernel, "shifts": shifts, "epoch_owner": epoch_owner, "valid_rows": valid_rows}


def correlate(field, kernel):
    half = KSIZE // 2
    padded = jnp.pad(field, half)
    summed = jnp.zeros_like(field)
    for row_off in range(KSIZE):
        for col_off in range(KSIZE):
            summed = summed + kernel[row_off, col_off] * padded[row_off:row_off + ROWS, col_off:col_off + COLS]
    return summed

def reference(images, variance, spread_kernel, shifts, epoch_owner, valid_rows):
    kernel_norm = spread_kernel / jnp.sum(spread_kernel)
    kernel_sq = kernel_norm * kernel_norm
    floor = 0.5 * jnp.sum(kernel_sq)
    row_ids = jnp.arange(ROWS, dtype=jnp.int32)[:, None]
    stacked = []
    for epoch in range(EPOCHS):
        slot = epoch_owner[epoch]
        exposure = images[slot]
        noise_var = variance[slot]
        usable = (row_ids >= valid_rows[epoch, 0]) & (row_ids < valid_rows[epoch, 1])
        weighted = jnp.where(usable, exposure / noise_var, jnp.float32(0.0))
        inverse = jnp.where(usable, 1.0 / noise_var, jnp.float32(0.0))
        pair = jnp.stack([correlate(weighted, kernel_norm), correlate(inverse, kernel_sq)])
        stacked.append(jnp.pad(pair, ((0, 0), (MAXS, MAXS), (MAXS, MAXS))))
    padded_all = jnp.stack(stacked)

    def one_velocity(shift):
        summed = jnp.zeros((2, ROWS, COLS), jnp.float32)
        for epoch in range(EPOCHS):
            start_row = (MAXS + shift[epoch, 0]).astype(jnp.int32)
            start_col = (MAXS + shift[epoch, 1]).astype(jnp.int32)
            summed = summed + lax.dynamic_slice(padded_all[epoch], (jnp.int32(0), start_row, start_col), (2, ROWS, COLS))
        return summed[0] / jnp.sqrt(jnp.maximum(summed[1], floor))
    return lax.map(one_velocity, shifts)
```

```python
import functools

import jax
import jax.numpy as jnp
from jax import lax
from jax.experimental import pallas as pl
from jax.experimental.pallas import tpu as pltpu
from jax.sharding import PartitionSpec as P

MAXS = 16
EPOCHS = 3
LANES = 128


def spread(value, axis, root):
    mine = lax.axis_index(axis) == root
    return lax.psum(jnp.where(mine, value, jnp.zeros_like(value)), axis)


def with_halo(value, sides, width):
    for axis, dim in sides:
        count, length = (lax.axis_size(axis), value.shape[dim])
        up = [(i, (i + 1) % count) for i in range(count - 1)]
        down = [(j, i) for i, j in up]
        last = lax.slice_in_dim(value, length - width, length, axis=dim)
        initial = lax.slice_in_dim(value, 0, width, axis=dim)
        before = lax.ppermute(last, axis, up)
        after = lax.ppermute(initial, axis, down)
        value = jnp.concatenate([before, value, after], axis=dim)
    return value


def band_matrix(kernels, ksize):
    inner = jnp.arange(128 + ksize - 1, dtype=jnp.int32)[:, None, None]
    outer = jnp.arange(128, dtype=jnp.int32)[None, :, None]
    offsets = jnp.arange(ksize, dtype=jnp.int32)[None, None, :]
    onehot = (inner - outer == offsets).astype(jnp.float32)
    return jnp.einsum("fkj,cdj->fkcd", kernels, onehot, precision=lax.Precision.HIGHEST)


def correlate_pair(extended, banded, ksize):
    half = ksize // 2
    height = extended.shape[1] - (ksize - 1)
    columns = extended.shape[2]
    blocks = columns // 128
    padded = jnp.pad(extended, ((0, 0), (0, 0), (half, 128 - half)))

    def add_row(offset, summed):
        row_band = lax.dynamic_slice_in_dim(padded, offset, height, 1)
        leading = row_band[:, :, :columns].reshape(2, height, blocks, 128)
        trailing = row_band[:, :, 128:].reshape(2, height, blocks, 128)[..., : ksize - 1]
        window = jnp.concatenate([leading, trailing], axis=3)
        weights = lax.dynamic_index_in_dim(banded, offset, 1, keepdims=False)
        return summed + jnp.einsum(
            "fhbc,fcd->fhbd", window, weights, precision=lax.Precision.HIGHEST
        )

    summed = lax.fori_loop(0, ksize, add_row, jnp.zeros((2, height, blocks, 128), jnp.float32))
    return summed.reshape(2, height, columns)


def stack_kernel(bands, band, shift_ref, where_ref, floor_ref, planes_ref, out_ref, held, sem):
    pieces, count, width, rows, _ = planes_ref.shape
    vel = pl.program_id(0)
    blocks = held.shape[1] - 2

    @pl.when(vel == 0)
    def _():
        copies = []
        for p in range(pieces):
            copies.append(
                pltpu.make_async_copy(
                    planes_ref.at[p],
                    held.at[:, pl.ds(1 + p * width, width), pl.ds(MAXS, rows), :],
                    sem.at[p],
                )
            )
        for c in copies:
            c.start()
        for f in range(count):
            held[f, 0] = jnp.zeros(held.shape[2:], jnp.float32)
            held[f, blocks + 1] = jnp.zeros(held.shape[2:], jnp.float32)
            edge = jnp.zeros((blocks, MAXS, LANES), jnp.float32)
            held[f, 1 : blocks + 1, 0:MAXS] = edge
            held[f, 1 : blocks + 1, MAXS + rows : 2 * MAXS + rows] = edge
        for c in copies:
            c.wait()

    floor = floor_ref[0]
    lane = lax.broadcasted_iota(jnp.int32, (band, LANES), 1)
    first_row = where_ref[0] + MAXS
    places = []
    for e in range(EPOCHS):
        dy = shift_ref[(vel * EPOCHS + e) * 2]
        dx = shift_ref[(vel * EPOCHS + e) * 2 + 1]
        back = jnp.where(dx < 0, 1, 0)
        offset = dx + back * LANES
        amount = jnp.where(offset == 0, 0, LANES - offset)
        keep = lane < LANES - offset
        places.append((first_row + dy, 1 - back, amount, keep))

    def rolled(e, f, b):
        row, start, amount, _ = places[e]
        return pltpu.roll(held[2 * e + f, start + b, pl.ds(row, band), :], amount, 1)

    def step(b, before):
        sums = [None, None]
        after = []
        for e in range(EPOCHS):
            for f in range(2):
                new = rolled(e, f, b + 1)
                term = jnp.where(places[e][3], before[2 * e + f], new)
                after.append(new)
                sums[f] = term if sums[f] is None else sums[f] + term
        value = sums[0] * lax.rsqrt(jnp.maximum(sums[1], floor))
        out_ref[0, :, pl.ds(pl.multiple_of(b * LANES, LANES), LANES)] = value
        return tuple(after)

    initial = tuple(rolled(e, f, 0) for e in range(EPOCHS) for f in range(2))
    lax.fori_loop(0, blocks, step, initial, unroll=4)


def stack(planes, shifts, floor, band, row_index):
    pieces, count, width, rows, _ = planes.shape
    velocities = shifts.shape[0]
    blocks = pieces * width
    smem = pl.BlockSpec(memory_space=pltpu.SMEM)
    return pl.pallas_call(
        functools.partial(stack_kernel, rows // band, band),
        grid=(velocities,),
        out_shape=jax.ShapeDtypeStruct((velocities, band, blocks * LANES), jnp.float32),
        in_specs=[smem, smem, smem, pl.BlockSpec(memory_space=pl.ANY)],
        out_specs=pl.BlockSpec((1, band, blocks * LANES), lambda v: (v, 0, 0)),
        scratch_shapes=[
            pltpu.VMEM((count, blocks + 2, rows + 2 * MAXS, LANES), jnp.float32),
            pltpu.SemaphoreType.DMA((pieces,)),
        ],
        name="stack",
    )(
        shifts.reshape(-1),
        (row_index * band).astype(jnp.int32).reshape(1),
        floor.reshape(1),
        planes,
    )


def local(images, variance, spread_kernel, shifts, epoch_owner, valid_rows):
    exposure = images[0]
    noise_var = variance[0]
    band_rows = exposure.shape[0]
    columns = exposure.shape[1]
    ksize = spread_kernel.shape[0]
    half = ksize // 2
    kernel_norm = spread_kernel / jnp.sum(spread_kernel)
    kernel_sq = kernel_norm * kernel_norm
    floor = 0.5 * jnp.sum(kernel_sq)
    vel_index = lax.axis_index("vel")
    row_index = lax.axis_index("rows")
    owned = epoch_owner == vel_index
    lower_row = jnp.sum(jnp.where(owned, valid_rows[:, 0], 0))
    upper_row = jnp.sum(jnp.where(owned, valid_rows[:, 1], 0))
    row_ids = row_index * band_rows + jnp.arange(band_rows, dtype=jnp.int32)[:, None]
    usable = (row_ids >= lower_row) & (row_ids < upper_row)
    weighted = jnp.where(usable, exposure / noise_var, jnp.float32(0.0))
    inverse = jnp.where(usable, 1.0 / noise_var, jnp.float32(0.0))
    fields_pair = jnp.stack([weighted, inverse])
    extended = with_halo(fields_pair, (("rows", 1),), half)
    banded = band_matrix(jnp.stack([kernel_norm, kernel_sq]), ksize)
    correlated = correlate_pair(extended, banded, ksize)
    narrow = jnp.stack([spread(correlated, "vel", epoch_owner[epoch]) for epoch in range(EPOCHS)])
    whole = lax.all_gather(narrow, "rows", axis=2, tiled=True)
    rows = whole.shape[2]
    planes = whole.reshape(2 * EPOCHS, rows, columns // LANES, LANES).transpose(0, 2, 1, 3)
    return stack(planes[None], shifts, floor, band_rows, row_index)


def solution(mesh):
    in_specs = (
        P(("fields", "vel"), "rows", None),
        P(("fields", "vel"), "rows", None),
        P(),
        P(("fields", "vel"), None, None),
        P("fields"),
        P("fields", None),
    )
    out_specs = P(("fields", "vel"), "rows", None)
    return jax.shard_map(local, mesh=mesh, in_specs=in_specs, out_specs=out_specs, check_vma=False)
```

```python
import functools

import jax
import jax.numpy as jnp
from jax import lax
from jax.experimental import pallas as pl
from jax.experimental.pallas import tpu as pltpu
from jax.sharding import PartitionSpec as P

MAXS = 16
EPOCHS = 3
LANES = 128


def split(value):
    high = value.astype(jnp.bfloat16)
    return high, (value - high.astype(jnp.float32)).astype(jnp.bfloat16)


def correlate_kernel(ksize, owner_ref, taps_ref, pieces_ref, out_ref, acc, left):
    bands, width, rows = pieces_ref.shape[1], pieces_ref.shape[2] - 1, pieces_ref.shape[3]
    height = bands * rows
    half = ksize // 2
    window = 2 * LANES
    lane = lax.broadcasted_iota(jnp.int32, (rows, LANES), 1)
    low = lane < LANES // 2
    for e in range(EPOCHS):
        slot = owner_ref[e]
        for r in range(bands):
            blocks = [pieces_ref[slot, r, b] for b in range(width + 1)]
            for b in range(width):
                after = blocks[b + 1]
                before = blocks[b - 1] if b else blocks[width]
                place = pl.ds((e * width + b) * height + r * rows, rows)
                own_high, own_low = split(blocks[b])
                side_high, side_low = split(jnp.where(low, after, before))
                left[place, 0:LANES] = own_high
                left[place, LANES:window] = side_high
                left[place, window : window + LANES] = own_low
                left[place, window + LANES : 2 * window] = side_low
    acc[...] = jnp.zeros_like(acc)

    def band(a):
        row = jnp.broadcast_to(taps_ref[a : a + 1, :], (window, window))
        return pltpu.roll(row, 0, 1, stride=1, stride_axis=0)[:, :LANES]

    for a in range(0, ksize, 2):
        count = min(2, ksize - a)
        weights = jnp.concatenate([band(a + i) for i in range(count)], axis=1)
        high, small = split(weights)
        for e in range(EPOCHS):
            place = pl.ds(e * width * height, width * height)
            values = left[place, :]
            product = jnp.dot(values[:, :window], high, preferred_element_type=jnp.float32)
            product += jnp.dot(values[:, window:], high, preferred_element_type=jnp.float32)
            product += jnp.dot(values[:, :window], small, preferred_element_type=jnp.float32)
            for i in range(count):
                shift = ksize - 1 - (a + i)
                part = product[:, i * LANES : (i + 1) * LANES].reshape(width, height, LANES)
                acc[e, :, shift : shift + height, :] += part
    out_ref[...] = acc[:, :, half : half + height, :]


def correlate(pieces, taps, epoch_owner, ksize):
    bands, width, rows = pieces.shape[1], pieces.shape[2] - 1, pieces.shape[3]
    height = bands * rows
    vmem = pl.BlockSpec(memory_space=pltpu.VMEM)
    return pl.pallas_call(
        functools.partial(correlate_kernel, ksize),
        out_shape=jax.ShapeDtypeStruct((EPOCHS, width, height, LANES), jnp.float32),
        in_specs=[pl.BlockSpec(memory_space=pltpu.SMEM), vmem, vmem],
        out_specs=vmem,
        scratch_shapes=[
            pltpu.VMEM((EPOCHS, width, height + ksize - 1, LANES), jnp.float32),
            pltpu.VMEM((EPOCHS * width * height, 4 * LANES), jnp.bfloat16),
        ],
        name="correlate",
    )(epoch_owner, taps, pieces)


def stack_kernel(bands, band, shift_ref, where_ref, floor_ref, planes_ref, out_ref, held, sem):
    pieces, count, width, rows, _ = planes_ref.shape
    vel = pl.program_id(0)
    blocks = held.shape[1] - 2

    @pl.when(vel == 0)
    def _():
        copies = []
        for p in range(pieces):
            copies.append(
                pltpu.make_async_copy(
                    planes_ref.at[p],
                    held.at[:, pl.ds(1 + p * width, width), pl.ds(MAXS, rows), :],
                    sem.at[p],
                )
            )
        for c in copies:
            c.start()
        for f in range(count):
            held[f, 0] = jnp.zeros(held.shape[2:], jnp.float32)
            held[f, blocks + 1] = jnp.zeros(held.shape[2:], jnp.float32)
            edge = jnp.zeros((blocks, MAXS, LANES), jnp.float32)
            held[f, 1 : blocks + 1, 0:MAXS] = edge
            held[f, 1 : blocks + 1, MAXS + rows : 2 * MAXS + rows] = edge
        for c in copies:
            c.wait()

    floor = floor_ref[0]
    lane = lax.broadcasted_iota(jnp.int32, (band, LANES), 1)
    first_row = where_ref[0] + MAXS
    places = []
    for e in range(EPOCHS):
        dy = shift_ref[(vel * EPOCHS + e) * 2]
        dx = shift_ref[(vel * EPOCHS + e) * 2 + 1]
        back = jnp.where(dx < 0, 1, 0)
        offset = dx + back * LANES
        amount = jnp.where(offset == 0, 0, LANES - offset)
        keep = lane < LANES - offset
        places.append((first_row + dy, 1 - back, amount, keep))

    def rolled(e, f, b):
        row, start, amount, _ = places[e]
        return pltpu.roll(held[f * EPOCHS + e, start + b, pl.ds(row, band), :], amount, 1)

    def step(b, before):
        sums = [None, None]
        after = []
        for e in range(EPOCHS):
            for f in range(2):
                new = rolled(e, f, b + 1)
                term = jnp.where(places[e][3], before[2 * e + f], new)
                after.append(new)
                sums[f] = term if sums[f] is None else sums[f] + term
        value = sums[0] * lax.rsqrt(jnp.maximum(sums[1], floor))
        out_ref[0, :, pl.ds(pl.multiple_of(b * LANES, LANES), LANES)] = value
        return tuple(after)

    initial = tuple(rolled(e, f, 0) for e in range(EPOCHS) for f in range(2))
    lax.fori_loop(0, blocks, step, initial, unroll=4)


def stack(planes, shifts, floor, band, row_index):
    pieces, count, width, rows, _ = planes.shape
    velocities = shifts.shape[0]
    blocks = pieces * width
    smem = pl.BlockSpec(memory_space=pltpu.SMEM)
    return pl.pallas_call(
        functools.partial(stack_kernel, rows // band, band),
        grid=(velocities,),
        out_shape=jax.ShapeDtypeStruct((velocities, band, blocks * LANES), jnp.float32),
        in_specs=[smem, smem, smem, pl.BlockSpec(memory_space=pl.ANY)],
        out_specs=pl.BlockSpec((1, band, blocks * LANES), lambda v: (v, 0, 0)),
        scratch_shapes=[
            pltpu.VMEM((count, blocks + 2, rows + 2 * MAXS, LANES), jnp.float32),
            pltpu.SemaphoreType.DMA((pieces,)),
        ],
        name="stack",
    )(
        shifts.reshape(-1),
        (row_index * band).astype(jnp.int32).reshape(1),
        floor.reshape(1),
        planes,
    )


def cut(plane, pieces):
    rows, columns = plane.shape
    blocks = columns // LANES
    tiles = plane.reshape(rows, blocks, LANES).transpose(1, 0, 2)
    own = tiles.reshape(pieces, blocks // pieces, rows, LANES)
    none = jnp.zeros((1, rows, LANES), jnp.float32)
    after = jnp.concatenate([own[1:, 0], none])
    before = jnp.concatenate([none, own[:-1, -1]])
    lane = jnp.arange(LANES, dtype=jnp.int32)
    sides = jnp.where(lane < LANES // 2, after, before)
    return jnp.concatenate([own, sides[:, None]], axis=1)


def local(images, variance, spread_kernel, shifts, epoch_owner, valid_rows):
    exposure = images[0]
    noise_var = variance[0]
    band_rows = exposure.shape[0]
    ksize = spread_kernel.shape[0]
    half = ksize // 2
    kernel_norm = spread_kernel / jnp.sum(spread_kernel)
    kernel_sq = kernel_norm * kernel_norm
    floor = 0.5 * jnp.sum(kernel_sq)
    slots = lax.axis_size("vel")
    vel_index = lax.axis_index("vel")
    row_index = lax.axis_index("rows")
    owned = epoch_owner == vel_index
    lower_row = jnp.sum(jnp.where(owned, valid_rows[:, 0], 0))
    upper_row = jnp.sum(jnp.where(owned, valid_rows[:, 1], 0))
    row_ids = row_index * band_rows + jnp.arange(band_rows, dtype=jnp.int32)[:, None]
    usable = (row_ids >= lower_row) & (row_ids < upper_row)
    weighted = jnp.where(usable, exposure / noise_var, jnp.float32(0.0))
    inverse = jnp.where(usable, 1.0 / noise_var, jnp.float32(0.0))
    sent = jnp.stack([cut(weighted, slots), cut(inverse, slots)], axis=1)
    sent = sent.reshape((-1,) + sent.shape[2:])
    got = lax.all_to_all(sent, ("vel", "rows"), 0, 0, tiled=True)
    got = got.reshape((slots, 2) + got.shape[1:])
    kernel = jnp.where(row_index == 0, kernel_norm, kernel_sq)
    taps = jnp.roll(jnp.pad(kernel[:, ::-1], ((0, 0), (0, 2 * LANES - ksize))), -half, axis=1)
    mine = correlate(got, taps, epoch_owner, ksize)
    planes = lax.all_gather(mine, ("vel", "rows"), axis=0)
    planes = planes.reshape((slots, 2 * EPOCHS) + planes.shape[2:])
    return stack(planes, shifts, floor, band_rows, row_index)


def solution(mesh):
    in_specs = (
        P(("fields", "vel"), "rows", None),
        P(("fields", "vel"), "rows", None),
        P(),
        P(("fields", "vel"), None, None),
        P("fields"),
        P("fields", None),
    )
    out_specs = P(("fields", "vel"), "rows", None)
    return jax.shard_map(local, mesh=mesh, in_specs=in_specs, out_specs=out_specs, check_vma=False)
```

```python
import functools

import jax
import jax.numpy as jnp
from jax import lax
from jax.experimental import pallas as pl
from jax.experimental.pallas import tpu as pltpu
from jax.sharding import PartitionSpec as P

MAXS = 16
EPOCHS = 3
LANES = 128


def split(value):
    high = value.astype(jnp.bfloat16)
    return high, (value - high.astype(jnp.float32)).astype(jnp.bfloat16)


def correlate_kernel(ksize, owner_ref, taps_ref, pieces_ref, out_ref, acc, left):
    bands, width, rows = pieces_ref.shape[1], pieces_ref.shape[2] - 1, pieces_ref.shape[3]
    height = bands * rows
    half = ksize // 2
    window = 2 * LANES
    lane = lax.broadcasted_iota(jnp.int32, (rows, LANES), 1)
    low = lane < LANES // 2
    for e in range(EPOCHS):
        slot = owner_ref[e]
        for r in range(bands):
            blocks = [pieces_ref[slot, r, b] for b in range(width + 1)]
            for b in range(width):
                after = blocks[b + 1]
                before = blocks[b - 1] if b else blocks[width]
                place = pl.ds((e * width + b) * height + r * rows, rows)
                own_high, own_low = split(blocks[b])
                side_high, side_low = split(jnp.where(low, after, before))
                left[place, 0:LANES] = own_high
                left[place, LANES:window] = side_high
                left[place, window : window + LANES] = own_low
                left[place, window + LANES : 2 * window] = side_low
    acc[...] = jnp.zeros_like(acc)

    def band(a):
        row = jnp.broadcast_to(taps_ref[a : a + 1, :], (window, window))
        return pltpu.roll(row, 0, 1, stride=1, stride_axis=0)[:, :LANES]

    for a in range(0, ksize, 2):
        count = min(2, ksize - a)
        weights = jnp.concatenate([band(a + i) for i in range(count)], axis=1)
        high, small = split(weights)
        for e in range(EPOCHS):
            place = pl.ds(e * width * height, width * height)
            values = left[place, :]
            product = jnp.dot(values[:, :window], high, preferred_element_type=jnp.float32)
            product += jnp.dot(values[:, window:], high, preferred_element_type=jnp.float32)
            product += jnp.dot(values[:, :window], small, preferred_element_type=jnp.float32)
            for i in range(count):
                shift = ksize - 1 - (a + i)
                part = product[:, i * LANES : (i + 1) * LANES].reshape(width, height, LANES)
                acc[e, :, shift : shift + height, :] += part
    out_ref[...] = acc[:, :, half : half + height, :]


def correlate(pieces, taps, epoch_owner, ksize):
    bands, width, rows = pieces.shape[1], pieces.shape[2] - 1, pieces.shape[3]
    height = bands * rows
    vmem = pl.BlockSpec(memory_space=pltpu.VMEM)
    return pl.pallas_call(
        functools.partial(correlate_kernel, ksize),
        out_shape=jax.ShapeDtypeStruct((EPOCHS, width, height, LANES), jnp.float32),
        in_specs=[pl.BlockSpec(memory_space=pltpu.SMEM), vmem, vmem],
        out_specs=vmem,
        scratch_shapes=[
            pltpu.VMEM((EPOCHS, width, height + ksize - 1, LANES), jnp.float32),
            pltpu.VMEM((EPOCHS * width * height, 4 * LANES), jnp.bfloat16),
        ],
        name="correlate",
    )(epoch_owner, taps, pieces)


MESH = pl.DeviceIdType.MESH


def ring_kernel(count, mine_ref, out_ref, own_sem, send_sem, recv_sem, pass_sem, take_sem):
    me, core = lax.axis_index("vel"), lax.axis_index("rows")
    other = 1 - core
    half = mine_ref.shape[1] // 2

    def index_at(position):
        position = (position + count) % count
        late = position // (count // 2)
        return (1 - late) * (2 * position) + late * (2 * (count - 1 - position) + 1)

    odd = me % 2
    position = (1 - odd) * (me // 2) + odd * (count - 1 - me // 2)
    ahead = [index_at(position + 1), index_at(position - 1)]

    barrier = pltpu.get_barrier_semaphore()
    for target in ({"vel": ahead[0]}, {"vel": ahead[1]}, {"rows": other}):
        pl.semaphore_signal(barrier, inc=1, device_id=target, device_id_type=MESH)
    pl.semaphore_wait(barrier, 3)

    own = pltpu.make_async_copy(mine_ref, out_ref.at[me, core], own_sem)
    own.start()
    sent, passed = {}, {}
    for s in range(count):
        for e in range(EPOCHS):
            for d in range(2):
                owner = index_at(position - s) if d == 0 else index_at(position + s)
                part = pl.ds(d * half, half)
                place = out_ref.at[owner, core, e, part]
                if s:
                    sent[s - 1, e, d].wait_recv()
                source = place if s else mine_ref.at[e, part]
                if s < count - 1:
                    copy = pltpu.make_async_remote_copy(
                        src_ref=source,
                        dst_ref=place,
                        send_sem=send_sem.at[s, e, d],
                        recv_sem=recv_sem.at[s, e, d],
                        device_id={"vel": ahead[d]},
                        device_id_type=MESH,
                    )
                    copy.start()
                    sent[s, e, d] = copy
                copy = pltpu.make_async_remote_copy(
                    src_ref=source,
                    dst_ref=place,
                    send_sem=pass_sem.at[s, e, d],
                    recv_sem=take_sem.at[s, e, d],
                    device_id={"rows": other},
                    device_id_type=MESH,
                )
                copy.start()
                passed[s, e, d] = copy
    for copy in sent.values():
        copy.wait_send()
    for copy in passed.values():
        copy.wait()
    own.wait()


def gather(mine):
    count = lax.axis_size("vel")
    return pl.pallas_call(
        functools.partial(ring_kernel, count),
        out_shape=jax.ShapeDtypeStruct((count, 2) + mine.shape, jnp.float32),
        in_specs=[pl.BlockSpec(memory_space=pltpu.VMEM)],
        out_specs=pl.BlockSpec(memory_space=pl.ANY),
        scratch_shapes=[
            pltpu.SemaphoreType.DMA,
            pltpu.SemaphoreType.DMA((count - 1, EPOCHS, 2)),
            pltpu.SemaphoreType.DMA((count - 1, EPOCHS, 2)),
            pltpu.SemaphoreType.DMA((count, EPOCHS, 2)),
            pltpu.SemaphoreType.DMA((count, EPOCHS, 2)),
        ],
        compiler_params=pltpu.CompilerParams(collective_id=0, has_side_effects=True),
        name="gather",
    )(mine)


def stack_kernel(bands, band, shift_ref, where_ref, floor_ref, planes_ref, out_ref, held, sem):
    pieces, count, width, rows, _ = planes_ref.shape
    vel = pl.program_id(0)
    blocks = held.shape[1] - 2

    @pl.when(vel == 0)
    def _():
        copies = []
        for p in range(pieces):
            copies.append(
                pltpu.make_async_copy(
                    planes_ref.at[p],
                    held.at[:, pl.ds(1 + p * width, width), pl.ds(MAXS, rows), :],
                    sem.at[p],
                )
            )
        for c in copies:
            c.start()
        for f in range(count):
            held[f, 0] = jnp.zeros(held.shape[2:], jnp.float32)
            held[f, blocks + 1] = jnp.zeros(held.shape[2:], jnp.float32)
            edge = jnp.zeros((blocks, MAXS, LANES), jnp.float32)
            held[f, 1 : blocks + 1, 0:MAXS] = edge
            held[f, 1 : blocks + 1, MAXS + rows : 2 * MAXS + rows] = edge
        for c in copies:
            c.wait()

    floor = floor_ref[0]
    lane = lax.broadcasted_iota(jnp.int32, (band, LANES), 1)
    first_row = where_ref[0] + MAXS
    places = []
    for e in range(EPOCHS):
        dy = shift_ref[(vel * EPOCHS + e) * 2]
        dx = shift_ref[(vel * EPOCHS + e) * 2 + 1]
        back = jnp.where(dx < 0, 1, 0)
        offset = dx + back * LANES
        amount = jnp.where(offset == 0, 0, LANES - offset)
        keep = lane < LANES - offset
        places.append((first_row + dy, 1 - back, amount, keep))

    def rolled(e, f, b):
        row, start, amount, _ = places[e]
        return pltpu.roll(held[f * EPOCHS + e, start + b, pl.ds(row, band), :], amount, 1)

    def step(b, before):
        sums = [None, None]
        after = []
        for e in range(EPOCHS):
            for f in range(2):
                new = rolled(e, f, b + 1)
                term = jnp.where(places[e][3], before[2 * e + f], new)
                after.append(new)
                sums[f] = term if sums[f] is None else sums[f] + term
        value = sums[0] * lax.rsqrt(jnp.maximum(sums[1], floor))
        out_ref[0, :, pl.ds(pl.multiple_of(b * LANES, LANES), LANES)] = value
        return tuple(after)

    initial = tuple(rolled(e, f, 0) for e in range(EPOCHS) for f in range(2))
    lax.fori_loop(0, blocks, step, initial, unroll=4)


def stack(planes, shifts, floor, band, row_index):
    pieces, count, width, rows, _ = planes.shape
    velocities = shifts.shape[0]
    blocks = pieces * width
    smem = pl.BlockSpec(memory_space=pltpu.SMEM)
    return pl.pallas_call(
        functools.partial(stack_kernel, rows // band, band),
        grid=(velocities,),
        out_shape=jax.ShapeDtypeStruct((velocities, band, blocks * LANES), jnp.float32),
        in_specs=[smem, smem, smem, pl.BlockSpec(memory_space=pl.ANY)],
        out_specs=pl.BlockSpec((1, band, blocks * LANES), lambda v: (v, 0, 0)),
        scratch_shapes=[
            pltpu.VMEM((count, blocks + 2, rows + 2 * MAXS, LANES), jnp.float32),
            pltpu.SemaphoreType.DMA((pieces,)),
        ],
        name="stack",
    )(
        shifts.reshape(-1),
        (row_index * band).astype(jnp.int32).reshape(1),
        floor.reshape(1),
        planes,
    )


def cut(plane, pieces):
    rows, columns = plane.shape
    blocks = columns // LANES
    tiles = plane.reshape(rows, blocks, LANES).transpose(1, 0, 2)
    own = tiles.reshape(pieces, blocks // pieces, rows, LANES)
    none = jnp.zeros((1, rows, LANES), jnp.float32)
    after = jnp.concatenate([own[1:, 0], none])
    before = jnp.concatenate([none, own[:-1, -1]])
    lane = jnp.arange(LANES, dtype=jnp.int32)
    sides = jnp.where(lane < LANES // 2, after, before)
    return jnp.concatenate([own, sides[:, None]], axis=1)


def local(images, variance, spread_kernel, shifts, epoch_owner, valid_rows):
    exposure = images[0]
    noise_var = variance[0]
    band_rows = exposure.shape[0]
    ksize = spread_kernel.shape[0]
    half = ksize // 2
    kernel_norm = spread_kernel / jnp.sum(spread_kernel)
    kernel_sq = kernel_norm * kernel_norm
    floor = 0.5 * jnp.sum(kernel_sq)
    slots = lax.axis_size("vel")
    vel_index = lax.axis_index("vel")
    row_index = lax.axis_index("rows")
    owned = epoch_owner == vel_index
    lower_row = jnp.sum(jnp.where(owned, valid_rows[:, 0], 0))
    upper_row = jnp.sum(jnp.where(owned, valid_rows[:, 1], 0))
    row_ids = row_index * band_rows + jnp.arange(band_rows, dtype=jnp.int32)[:, None]
    usable = (row_ids >= lower_row) & (row_ids < upper_row)
    weighted = jnp.where(usable, exposure / noise_var, jnp.float32(0.0))
    inverse = jnp.where(usable, 1.0 / noise_var, jnp.float32(0.0))
    sent = jnp.stack([cut(weighted, slots), cut(inverse, slots)], axis=1)
    sent = sent.reshape((-1,) + sent.shape[2:])
    got = lax.all_to_all(sent, ("vel", "rows"), 0, 0, tiled=True)
    got = got.reshape((slots, 2) + got.shape[1:])
    kernel = jnp.where(row_index == 0, kernel_norm, kernel_sq)
    taps = jnp.roll(jnp.pad(kernel[:, ::-1], ((0, 0), (0, 2 * LANES - ksize))), -half, axis=1)
    mine = correlate(got, taps, epoch_owner, ksize)
    planes = gather(mine)
    planes = planes.reshape((slots, 2 * EPOCHS) + planes.shape[3:])
    return stack(planes, shifts, floor, band_rows, row_index)


def solution(mesh):
    in_specs = (
        P(("fields", "vel"), "rows", None),
        P(("fields", "vel"), "rows", None),
        P(),
        P(("fields", "vel"), None, None),
        P("fields"),
        P("fields", None),
    )
    out_specs = P(("fields", "vel"), "rows", None)
    return jax.shard_map(local, mesh=mesh, in_specs=in_specs, out_specs=out_specs, check_vma=False)
```

```python
import functools

import jax
import jax.numpy as jnp
from jax import lax
from jax.experimental import pallas as pl
from jax.experimental.pallas import tpu as pltpu
from jax.sharding import PartitionSpec as P

MAXS = 16
EPOCHS = 3
LANES = 128


def split(value):
    high = value.astype(jnp.bfloat16)
    return high, (value - high.astype(jnp.float32)).astype(jnp.bfloat16)


def correlate_kernel(ksize, owner_ref, taps_ref, pieces_ref, out_ref, acc, left):
    bands, width, rows = pieces_ref.shape[1], pieces_ref.shape[2] - 1, pieces_ref.shape[3]
    height = bands * rows
    half = ksize // 2
    window = 2 * LANES
    lane = lax.broadcasted_iota(jnp.int32, (rows, LANES), 1)
    low = lane < LANES // 2
    for e in range(EPOCHS):
        slot = owner_ref[e]
        for r in range(bands):
            blocks = [pieces_ref[slot, r, b] for b in range(width + 1)]
            for b in range(width):
                after = blocks[b + 1]
                before = blocks[b - 1] if b else blocks[width]
                place = pl.ds((e * width + b) * height + r * rows, rows)
                own_high, own_low = split(blocks[b])
                side_high, side_low = split(jnp.where(low, after, before))
                left[place, 0:LANES] = own_high
                left[place, LANES:window] = side_high
                left[place, window : window + LANES] = own_low
                left[place, window + LANES : 2 * window] = side_low
    acc[...] = jnp.zeros_like(acc)

    def band(a):
        row = jnp.broadcast_to(taps_ref[a : a + 1, :], (window, window))
        return pltpu.roll(row, 0, 1, stride=1, stride_axis=0)[:, :LANES]

    for a in range(0, ksize, 2):
        count = min(2, ksize - a)
        weights = jnp.concatenate([band(a + i) for i in range(count)], axis=1)
        high, small = split(weights)
        for e in range(EPOCHS):
            place = pl.ds(e * width * height, width * height)
            values = left[place, :]
            product = jnp.dot(values[:, :window], high, preferred_element_type=jnp.float32)
            product += jnp.dot(values[:, window:], high, preferred_element_type=jnp.float32)
            product += jnp.dot(values[:, :window], small, preferred_element_type=jnp.float32)
            for i in range(count):
                shift = ksize - 1 - (a + i)
                part = product[:, i * LANES : (i + 1) * LANES].reshape(width, height, LANES)
                acc[e, :, shift : shift + height, :] += part
    out_ref[...] = acc[:, :, half : half + height, :]


def correlate(pieces, taps, epoch_owner, ksize):
    bands, width, rows = pieces.shape[1], pieces.shape[2] - 1, pieces.shape[3]
    height = bands * rows
    vmem = pl.BlockSpec(memory_space=pltpu.VMEM)
    return pl.pallas_call(
        functools.partial(correlate_kernel, ksize),
        out_shape=jax.ShapeDtypeStruct((EPOCHS, width, height, LANES), jnp.float32),
        in_specs=[pl.BlockSpec(memory_space=pltpu.SMEM), vmem, vmem],
        out_specs=vmem,
        scratch_shapes=[
            pltpu.VMEM((EPOCHS, width, height + ksize - 1, LANES), jnp.float32),
            pltpu.VMEM((EPOCHS * width * height, 4 * LANES), jnp.bfloat16),
        ],
        name="correlate",
    )(epoch_owner, taps, pieces)


MESH = pl.DeviceIdType.MESH


def ring_kernel(count, mine_ref, out_ref, own_sem, send_sem, recv_sem, pass_sem, take_sem):
    me, core = lax.axis_index("vel"), lax.axis_index("rows")
    other = 1 - core
    half = mine_ref.shape[1] // 2

    def index_at(position):
        position = (position + count) % count
        late = position // (count // 2)
        return (1 - late) * (2 * position) + late * (2 * (count - 1 - position) + 1)

    odd = me % 2
    position = (1 - odd) * (me // 2) + odd * (count - 1 - me // 2)
    ahead = [index_at(position + 1), index_at(position - 1)]

    barrier = pltpu.get_barrier_semaphore()
    for target in ({"vel": ahead[0]}, {"vel": ahead[1]}, {"rows": other}):
        pl.semaphore_signal(barrier, inc=1, device_id=target, device_id_type=MESH)
    pl.semaphore_wait(barrier, 3)

    own = pltpu.make_async_copy(mine_ref, out_ref.at[me, core], own_sem)
    own.start()
    sent, passed = {}, {}
    for s in range(count):
        for e in range(EPOCHS):
            for d in range(2):
                owner = index_at(position - s) if d == 0 else index_at(position + s)
                part = pl.ds(d * half, half)
                place = out_ref.at[owner, core, e, part]
                if s:
                    sent[s - 1, e, d].wait_recv()
                source = place if s else mine_ref.at[e, part]
                if s < count - 1:
                    copy = pltpu.make_async_remote_copy(
                        src_ref=source,
                        dst_ref=place,
                        send_sem=send_sem.at[s, e, d],
                        recv_sem=recv_sem.at[s, e, d],
                        device_id={"vel": ahead[d]},
                        device_id_type=MESH,
                    )
                    copy.start()
                    sent[s, e, d] = copy
                copy = pltpu.make_async_remote_copy(
                    src_ref=source,
                    dst_ref=place,
                    send_sem=pass_sem.at[s, e, d],
                    recv_sem=take_sem.at[s, e, d],
                    device_id={"rows": other},
                    device_id_type=MESH,
                )
                copy.start()
                passed[s, e, d] = copy
    for copy in sent.values():
        copy.wait_send()
    for copy in passed.values():
        copy.wait()
    own.wait()


def gather(mine):
    count = lax.axis_size("vel")
    return pl.pallas_call(
        functools.partial(ring_kernel, count),
        out_shape=jax.ShapeDtypeStruct((count, 2) + mine.shape, jnp.float32),
        in_specs=[pl.BlockSpec(memory_space=pltpu.VMEM)],
        out_specs=pl.BlockSpec(memory_space=pl.ANY),
        scratch_shapes=[
            pltpu.SemaphoreType.DMA,
            pltpu.SemaphoreType.DMA((count - 1, EPOCHS, 2)),
            pltpu.SemaphoreType.DMA((count - 1, EPOCHS, 2)),
            pltpu.SemaphoreType.DMA((count, EPOCHS, 2)),
            pltpu.SemaphoreType.DMA((count, EPOCHS, 2)),
        ],
        compiler_params=pltpu.CompilerParams(collective_id=0, has_side_effects=True),
        name="gather",
    )(mine)


def stack_kernel(bands, band, shift_ref, where_ref, floor_ref, planes_ref, out_ref, held, sem):
    pieces, count, width, rows, _ = planes_ref.shape
    vel = pl.program_id(0)
    blocks = held.shape[1] - 2

    @pl.when(vel == 0)
    def _():
        copies = []
        for p in range(pieces):
            copies.append(
                pltpu.make_async_copy(
                    planes_ref.at[p],
                    held.at[:, pl.ds(1 + p * width, width), pl.ds(MAXS, rows), :],
                    sem.at[p],
                )
            )
        for c in copies:
            c.start()
        for f in range(count):
            held[f, 0] = jnp.zeros(held.shape[2:], jnp.float32)
            held[f, blocks + 1] = jnp.zeros(held.shape[2:], jnp.float32)
            edge = jnp.zeros((blocks, MAXS, LANES), jnp.float32)
            held[f, 1 : blocks + 1, 0:MAXS] = edge
            held[f, 1 : blocks + 1, MAXS + rows : 2 * MAXS + rows] = edge
        for c in copies:
            c.wait()

    floor = floor_ref[0]
    lane = lax.broadcasted_iota(jnp.int32, (band, LANES), 1)
    first_row = where_ref[0] + MAXS
    places = []
    for e in range(EPOCHS):
        dy = shift_ref[(vel * EPOCHS + e) * 2]
        dx = shift_ref[(vel * EPOCHS + e) * 2 + 1]
        back = jnp.where(dx < 0, 1, 0)
        offset = dx + back * LANES
        amount = jnp.where(offset == 0, 0, LANES - offset)
        keep = lane < LANES - offset
        places.append((first_row + dy, 1 - back, amount, keep))

    def rolled(e, f, b):
        row, start, amount, _ = places[e]
        return pltpu.roll(held[f * EPOCHS + e, start + b, pl.ds(row, band), :], amount, 1)

    def step(b, before):
        sums = [None, None]
        after = []
        for e in range(EPOCHS):
            for f in range(2):
                new = rolled(e, f, b + 1)
                term = jnp.where(places[e][3], before[2 * e + f], new)
                after.append(new)
                sums[f] = term if sums[f] is None else sums[f] + term
        value = sums[0] * lax.rsqrt(jnp.maximum(sums[1], floor))
        out_ref[0, :, pl.ds(pl.multiple_of(b * LANES, LANES), LANES)] = value
        return tuple(after)

    initial = tuple(rolled(e, f, 0) for e in range(EPOCHS) for f in range(2))
    lax.fori_loop(0, blocks, step, initial, unroll=blocks)


def stack(planes, shifts, floor, band, row_index):
    pieces, count, width, rows, _ = planes.shape
    velocities = shifts.shape[0]
    blocks = pieces * width
    smem = pl.BlockSpec(memory_space=pltpu.SMEM)
    return pl.pallas_call(
        functools.partial(stack_kernel, rows // band, band),
        grid=(velocities,),
        out_shape=jax.ShapeDtypeStruct((velocities, band, blocks * LANES), jnp.float32),
        in_specs=[smem, smem, smem, pl.BlockSpec(memory_space=pl.ANY)],
        out_specs=pl.BlockSpec((1, band, blocks * LANES), lambda v: (v, 0, 0)),
        scratch_shapes=[
            pltpu.VMEM((count, blocks + 2, rows + 2 * MAXS, LANES), jnp.float32),
            pltpu.SemaphoreType.DMA((pieces,)),
        ],
        name="stack",
    )(
        shifts.reshape(-1),
        (row_index * band).astype(jnp.int32).reshape(1),
        floor.reshape(1),
        planes,
    )


def cut(plane, pieces):
    rows, columns = plane.shape
    blocks = columns // LANES
    tiles = plane.reshape(rows, blocks, LANES).transpose(1, 0, 2)
    own = tiles.reshape(pieces, blocks // pieces, rows, LANES)
    none = jnp.zeros((1, rows, LANES), jnp.float32)
    after = jnp.concatenate([own[1:, 0], none])
    before = jnp.concatenate([none, own[:-1, -1]])
    lane = jnp.arange(LANES, dtype=jnp.int32)
    sides = jnp.where(lane < LANES // 2, after, before)
    return jnp.concatenate([own, sides[:, None]], axis=1)


def local(images, variance, spread_kernel, shifts, epoch_owner, valid_rows):
    exposure = images[0]
    noise_var = variance[0]
    band_rows = exposure.shape[0]
    ksize = spread_kernel.shape[0]
    half = ksize // 2
    kernel_norm = spread_kernel / jnp.sum(spread_kernel)
    kernel_sq = kernel_norm * kernel_norm
    floor = 0.5 * jnp.sum(kernel_sq)
    slots = lax.axis_size("vel")
    vel_index = lax.axis_index("vel")
    row_index = lax.axis_index("rows")
    owned = epoch_owner == vel_index
    lower_row = jnp.sum(jnp.where(owned, valid_rows[:, 0], 0))
    upper_row = jnp.sum(jnp.where(owned, valid_rows[:, 1], 0))
    row_ids = row_index * band_rows + jnp.arange(band_rows, dtype=jnp.int32)[:, None]
    usable = (row_ids >= lower_row) & (row_ids < upper_row)
    weighted = jnp.where(usable, exposure / noise_var, jnp.float32(0.0))
    inverse = jnp.where(usable, 1.0 / noise_var, jnp.float32(0.0))
    sent = jnp.stack([cut(weighted, slots), cut(inverse, slots)], axis=1)
    sent = sent.reshape((-1,) + sent.shape[2:])
    got = lax.all_to_all(sent, ("vel", "rows"), 0, 0, tiled=True)
    got = got.reshape((slots, 2) + got.shape[1:])
    kernel = jnp.where(row_index == 0, kernel_norm, kernel_sq)
    taps = jnp.roll(jnp.pad(kernel[:, ::-1], ((0, 0), (0, 2 * LANES - ksize))), -half, axis=1)
    mine = correlate(got, taps, epoch_owner, ksize)
    planes = gather(mine)
    planes = planes.reshape((slots, 2 * EPOCHS) + planes.shape[3:])
    return stack(planes, shifts, floor, band_rows, row_index)


def solution(mesh):
    in_specs = (
        P(("fields", "vel"), "rows", None),
        P(("fields", "vel"), "rows", None),
        P(),
        P(("fields", "vel"), None, None),
        P("fields"),
        P("fields", None),
    )
    out_specs = P(("fields", "vel"), "rows", None)
    return jax.shard_map(local, mesh=mesh, in_specs=in_specs, out_specs=out_specs, check_vma=False)
```
